256 devices in a mesh: ctx: 2 (over core), exp: 8 (over z), tp: 16 (over y, x).
Axes of the slice: x: 4, y: 4, z: 8, core: 2. Of those that a mesh axis runs over, the one named last changes fastest.
Arguments:
- conv_in: bfloat16 [8, 256, 4096], P('exp', 'ctx', 'tp'), may hold values from -6 to 6
- gate_in: bfloat16 [8, 256, 4096], P('exp', 'ctx', 'tp'), may hold values from -6 to 6
- residual: bfloat16 [8, 256, 2048], P('exp', 'ctx'), may hold values from -6 to 6
- conv_weight: float32 [4, 4096], P(None, 'tp'), may hold values from -3 to 3
- conv_bias: float32 [4096], P('tp'), may hold values from -3 to 3
- proj_weight: bfloat16 [4096, 288], P('tp'), may hold values from -0.09375 to 0.09375
- step_weight: bfloat16 [256, 4096], P(None, 'tp'), may hold values from -0.375 to 0.375
- step_bias: float32 [4096], P('tp'), may hold values from -6 to -2
- decay_log: float32 [16, 4096], P(None, 'tp'), may hold values from -3 to 2
- skip_gain: float32 [4096], P('tp'), may hold values from 0.5 to 1.5
- out_weight: bfloat16 [4096, 2048], P('tp'), may hold values from -0.09375 to 0.09375
- norm_gain: float32 [2048], replicated, may hold values from 0.5 to 1.5
- expert_ids: int32 [8, 256, 2], P('exp', 'ctx'), may hold values from 0 to 7, all different within a row; in each aligned block of 128 rows (0 to 127, 128 to 255, ..., all dimensions but the last counted through in order) at most 64 rows name the same one
- route_gates: float32 [8, 256, 2], P('exp', 'ctx'), may hold values from 0.2 to 1
- expert_weight: bfloat16 [8, 3, 2048, 14336], P('exp', None, None, ('ctx', 'tp')), may hold values from -0.125 to 0.125
Outputs:
- layer_out: bfloat16 [8, 256, 2048], P('exp', 'ctx', 'tp')
The draws below stay inside these ranges and needn't reach their ends.
Inputs may be any that keep to these rules, and one draw needn't show every extreme that they name: `expert_ids`: the 2 picks of a token differ. Among the picks of the 128 tokens of one sequence block, no expert is named more than 64 times, and in some block one expert is named exactly 64 times.
All inputs are finite; a program needn't handle non-finite values.
Results may differ from the reference program's by a relative error of at most 0.015.
Values may be sent and summed in bfloat16 or wider, within the bound.
A program may use at most 128 MiB of HBM per device.

```python
import math
import jax
import jax.numpy as jnp
import numpy as np
from jax import lax

D = 2048
INNER = 4096
STATE = 16
DT_RANK = 256
CONV = 4
FF = 14336
TOP = 2
TOK_DEV = 128
CAP = 64
EXPERTS = 8
SEQS = 8
LEN = 256


def block_levels(own_key, dims, pieces, smallest, top_value):
    def one(axis_at, blocks):
        heights = jax.random.uniform(jax.random.fold_in(jax.random.fold_in(own_key, 6), axis_at), (blocks,), jnp.float32, smallest / len(pieces), top_value / len(pieces))
        return jnp.repeat(jnp.exp(heights), dims[axis_at] // blocks).reshape((-1,) + (1,) * (len(dims) - axis_at - 1))

    loudness = one(*pieces[0])
    for cut in pieces[1:]:
        loudness = loudness * one(*cut)
    return loudness


def assign_block(own_key, own, number, rows, count, top, bound, lean):
    sequence = jax.random.permutation(own_key, count)
    crowded, usual = portions_of(count, rows * top, bound, lean, True), portions_of(count, rows * top, bound, lean, False)
    places = jnp.arange(count)

    def named(lengths, turn):
        used = int((lengths > 0).sum())
        fixed = max(1, used // 4)
        moved = fixed + (places - fixed + turn * (used - fixed)) % max(1, count - fixed)
        return jnp.zeros((count,), jnp.int32).at[sequence[jnp.where(places < fixed, places, moved)]].set(jnp.asarray(lengths, jnp.int32))

    lengths = jnp.where(number % 4 == 0, named(crowded, number // 4), named(usual, number - number // 4 - 1))
    mixed = jax.random.permutation(jax.random.fold_in(own, 3), count)
    source_of, sink = mixed[0:count // 2 * 2:2], mixed[1:count // 2 * 2:2]
    room = jnp.minimum(lengths[source_of] - 1, bound - lengths[sink]) // 2
    room = jnp.where((source_of == sequence[0]) | (sink == sequence[0]) | (lengths[sink] == 0), 0, jnp.maximum(room, 0))
    moved = jax.random.randint(jax.random.fold_in(own, 4), (count // 2,), 0, 1 << 20) % (room + 1)
    lengths = lengths.at[source_of].add(-moved).at[sink].add(moved)
    members = jnp.searchsorted(jnp.cumsum(lengths), jnp.arange(rows * top), side="right").astype(jnp.int32)
    grid = members.reshape(top, rows).T
    grid = grid[jax.random.permutation(jax.random.fold_in(own, 1), rows)]
    turn = jax.random.randint(jax.random.fold_in(own, 2), (rows, 1), 0, top)
    return jnp.take_along_axis(grid, (jnp.arange(top)[None, :] + turn) % top, axis=1)


def portions_of(amount, total, limit, skew, full):
    portions = [(1 << 20) // math.isqrt(grade ** skew) + 1 for grade in range(1, amount + 1)]
    largest = limit if full else min(limit, max(-(-total // amount), total * portions[0] // sum(portions)))
    least = 1 if total - largest >= amount - 1 else 0
    given, surplus = [largest] + [least] * (amount - 1), total - largest - least * (amount - 1)
    while surplus > 0:
        movable = [i for i in range(1, amount) if given[i] < largest] or [i for i in range(1, amount) if given[i] < limit]
        pool, left = sum([portions[i] for i in movable]), surplus
        for i in movable:
            extra = min(limit - given[i], max(1, left * portions[i] // pool), surplus)
            given[i] = given[i] + extra
            surplus = surplus - extra
    return np.array(given)


def centred(own_key, shape, width, limit, pieces=(), kind=jnp.bfloat16):
    level = block_levels(own_key, shape, pieces, -0.22, 0.18) if pieces else 1.0
    array = jax.random.normal(own_key, shape, jnp.float32) * width * level
    return jnp.minimum(jnp.maximum(array, -limit), limit).astype(kind)


def setup_inputs(seed: int = 0) -> dict:
    streams_of = jax.random.split(jax.random.key(seed), 16)
    conv_in = centred(streams_of[0], (SEQS, LEN, INNER), 1.0, 6.0, ((0, 8), (1, 2), (2, 16)))
    gate_in = centred(streams_of[1], (SEQS, LEN, INNER), 1.0, 6.0, ((0, 8), (1, 2), (2, 16)))
    residual = centred(streams_of[2], (SEQS, LEN, D), 1.0, 6.0, ((0, 8), (1, 2)))
    conv_weight = centred(streams_of[3], (CONV, INNER), CONV ** -0.5, 3.0, ((1, 16),), jnp.float32)
    conv_bias = centred(streams_of[4], (INNER,), 0.5, 3.0, ((0, 16),), jnp.float32)
    proj_weight = centred(streams_of[5], (INNER, DT_RANK + 2 * STATE), INNER ** -0.5, 0.09375, ((0, 16),))
    step_weight = centred(streams_of[6], (DT_RANK, INNER), DT_RANK ** -0.5, 0.375, ((1, 16),))
    step_bias = jnp.clip(-6.0 + 4.0 * jax.random.uniform(streams_of[7], (INNER,), jnp.float32) ** block_levels(streams_of[7], (INNER,), ((0, 16),), -0.2, 0.2), -6.0, -2.0)
    decay_log = jnp.clip(-3.0 + 5.0 * jax.random.uniform(streams_of[8], (STATE, INNER), jnp.float32) ** block_levels(streams_of[8], (STATE, INNER), ((1, 16),), -0.2, 0.2), -3.0, 2.0)
    skip_gain = jnp.clip(0.5 + 1.0 * jax.random.uniform(streams_of[9], (INNER,), jnp.float32) ** block_levels(streams_of[9], (INNER,), ((0, 16),), -0.2, 0.2), 0.5, 1.5)
    out_weight = centred(streams_of[10], (INNER, D), INNER ** -0.5, 0.09375, ((0, 16),))
    norm_gain = jnp.clip(1.0 + 0.1 * jax.random.normal(streams_of[11], (D,), jnp.float32), 0.5, 1.5)
    expert_ids_keys = jax.random.split(jax.random.fold_in(streams_of[12], 1), SEQS * LEN // TOK_DEV)
    expert_ids_turns = jax.random.permutation(jax.random.fold_in(streams_of[12], 3), SEQS * LEN // TOK_DEV)
    expert_ids = jax.vmap(lambda own, number: assign_block(jax.random.fold_in(streams_of[12], 2), own, number, TOK_DEV, EXPERTS, TOP, CAP, 2))(expert_ids_keys, expert_ids_turns).reshape((SEQS, LEN, TOP))
    route_gates = jnp.clip(0.2 + 0.8 * jax.random.uniform(streams_of[13], (SEQS, LEN, TOP), jnp.float32) ** block_levels(streams_of[13], (SEQS, LEN, TOP), ((0, 8), (1, 2)), -0.2, 0.2), 0.2, 1.0)
    expert_weight = centred(streams_of[14], (EXPERTS, 3, D, FF), D ** -0.5, 0.125, ((0, 8), (3, 32)))
    return dict(conv_in=conv_in, gate_in=gate_in, residual=residual, conv_weight=conv_weight, conv_bias=conv_bias, proj_weight=proj_weight, step_weight=step_weight, step_bias=step_bias, decay_log=decay_log, skip_gain=skip_gain, out_weight=out_weight, norm_gain=norm_gain, expert_ids=expert_ids, route_gates=route_gates, expert_weight=expert_weight)


def reference(conv_in, gate_in, residual, conv_weight, conv_bias, proj_weight, step_weight, step_bias, decay_log, skip_gain, out_weight, norm_gain, expert_ids, route_gates, expert_weight):
    highest = lax.Precision.HIGHEST
    seq_count = conv_in.shape[0]
    seq_length = conv_in.shape[1]
    padded = jnp.pad(conv_in.astype(jnp.float32), ((0, 0), (CONV - 1, 0), (0, 0)))
    convolved = conv_bias[None, None, :] + sum((conv_weight[k][None, None, :] * padded[:, k:k + seq_length] for k in range(CONV)))
    xconv = jax.nn.silu(convolved).astype(jnp.bfloat16)
    projected = jnp.dot(xconv.reshape(seq_count * seq_length, INNER), proj_weight, preferred_element_type=jnp.float32)
    projected = projected.reshape(seq_count, seq_length, DT_RANK + 2 * STATE)
    rank_part = projected[..., :DT_RANK].astype(jnp.bfloat16)
    input_map = projected[..., DT_RANK:DT_RANK + STATE]
    output_map = projected[..., DT_RANK + STATE:]
    step_sizes = jnp.dot(rank_part.reshape(seq_count * seq_length, DT_RANK), step_weight, preferred_element_type=jnp.float32)
    step_sizes = jax.nn.softplus(step_sizes.reshape(seq_count, seq_length, INNER) + step_bias)
    decay_rates = -jnp.exp(decay_log)
    xfloat = xconv.astype(jnp.float32)

    def advance(state, inputs):
        step_now, value_now, in_now, out_now = inputs
        state = jnp.exp(step_now[:, None, :] * decay_rates[None]) * state + (step_now * value_now)[:, None, :] * in_now[:, :, None]
        return (state, jnp.einsum('sn,snc->sc', out_now, state, precision=highest))
    initial = jnp.zeros((seq_count, STATE, INNER), jnp.float32)
    _, scanned = lax.scan(advance, initial, (jnp.swapaxes(step_sizes, 0, 1), jnp.swapaxes(xfloat, 0, 1), jnp.swapaxes(input_map, 0, 1), jnp.swapaxes(output_map, 0, 1)))
    outputs = jnp.swapaxes(scanned, 0, 1) + skip_gain * xfloat
    gated = (outputs * jax.nn.silu(gate_in.astype(jnp.float32))).astype(jnp.bfloat16)
    mixed = jnp.dot(gated.reshape(seq_count * seq_length, INNER), out_weight, preferred_element_type=jnp.float32)
    stream = (residual.reshape(seq_count * seq_length, D).astype(jnp.float32) + mixed).astype(jnp.bfloat16)
    sfloat = stream.astype(jnp.float32)
    meansq = lax.optimization_barrier(jnp.mean(sfloat * sfloat, axis=1, keepdims=True))
    normed = (sfloat * lax.rsqrt(meansq + 1e-06) * norm_gain).astype(jnp.bfloat16)
    block_count = seq_count * seq_length // TOK_DEV
    picks = expert_ids.reshape(block_count, TOK_DEV, TOP)
    onehot = (picks[..., None] == jnp.arange(EXPERTS, dtype=jnp.int32)).astype(jnp.int32)
    flat_hot = onehot.reshape(block_count, TOK_DEV * TOP, EXPERTS)
    ranks = jnp.cumsum(flat_hot, axis=1) - 1
    within = lax.optimization_barrier(jnp.sum(ranks * flat_hot, axis=2)).reshape(block_count, TOK_DEV, TOP)
    places = picks * CAP + within
    table = (places[..., None] == jnp.arange(EXPERTS * CAP, dtype=jnp.int32)).astype(jnp.float32)
    chooser = lax.optimization_barrier(jnp.sum(table, axis=2))
    blender = lax.optimization_barrier(jnp.sum(table * route_gates.reshape(block_count, TOK_DEV, TOP)[..., None], axis=2))
    buffers = jnp.einsum('btm,btd->bmd', chooser, normed.reshape(block_count, TOK_DEV, D).astype(jnp.float32), precision=highest).astype(jnp.bfloat16)
    grouped = jnp.swapaxes(buffers.reshape(block_count, EXPERTS, CAP, D), 0, 1).reshape(EXPERTS, block_count * CAP, D)

    def expert(inputs):
        rows_in, weights = inputs
        gate_part = jnp.dot(rows_in, weights[0], preferred_element_type=jnp.float32)
        up_part = jnp.dot(rows_in, weights[1], preferred_element_type=jnp.float32)
        hidden = (jax.nn.silu(gate_part) * up_part).astype(jnp.bfloat16)
        return lax.dot_general(hidden, weights[2], (((1,), (1,)), ((), ())), preferred_element_type=jnp.float32).astype(jnp.bfloat16)
    results = lax.map(expert, (grouped, expert_weight))
    back = jnp.swapaxes(results.reshape(EXPERTS, block_count, CAP, D), 0, 1).reshape(block_count, EXPERTS * CAP, D)
    moe = jnp.einsum('btm,bmd->btd', blender, back.astype(jnp.float32), precision=highest)
    final = (sfloat.reshape(block_count, TOK_DEV, D) + moe).astype(jnp.bfloat16)
    return final.reshape(seq_count, seq_length, D)
```

```python
import functools

import jax
import jax.numpy as jnp
from jax import lax
from jax.experimental import pallas as pl
from jax.experimental.pallas import tpu as pltpu
from jax.sharding import PartitionSpec as P

F32, BF16 = jnp.float32, jnp.bfloat16
D = 2048
STATE = 16
RANK = 256
CAP = 64
TOKENS = 128
CHANNELS = 256
HIDDEN = 448
SIDE = 4
TP = 16
EXP = 8
ROWS = EXP * CAP
GROUP = ROWS // 2
NEAR = (0, 1, 7, 2, 6, 3, 5, 4)
PEERS = [(dy, dx) for dy in (2, 1, 3, 0) for dx in (2, 1, 3, 0) if (dy, dx) != (0, 0)]


def dot(a, b, dims=((1,), (0,))):
    return lax.dot_general(a, b, (dims, ((), ())), preferred_element_type=F32)


def silu(v):
    return v * jax.nn.sigmoid(v)


def kernel(
    conv_in, gate_in, residual, conv_w, conv_b, proj_w, step_w, step_b, decay_log, skip, out_w, gain, ids, gates, experts,
    out,
    halo, ext, psend, precv, pall, mb, steps, driven, ys, hend, hstart, ow, res, osend, orecv, picked, xs, xn, wv, hid, rsend, rrecv, ret_send, ret,
    local_sem, ctx_send, ctx_recv, p_send, p_recv, a_send, a_recv, o_send, o_recv, z_send, z_recv, g_send, g_recv, r_send, r_recv, b_send, b_recv,
):
    core, z, tp = lax.axis_index("ctx"), lax.axis_index("exp"), lax.axis_index("tp")
    my_y, my_x = tp // SIDE, lax.rem(tp, SIDE)
    partner = {"ctx": 1 - core}

    def peer_of(dy, dx):
        return lax.rem(my_y + dy, SIDE) * SIDE + lax.rem(my_x + dx, SIDE)

    def remote(src, dst, ss, rs, device):
        return pltpu.make_async_remote_copy(
            src_ref=src, dst_ref=dst, send_sem=ss, recv_sem=rs, device_id=device, device_id_type=pl.DeviceIdType.MESH
        )

    my_lanes = pl.ds(pl.multiple_of(tp * 128, 128), 128)
    load_ow = pltpu.make_async_copy(out_w, ow, local_sem.at[0])
    load_res = pltpu.make_async_copy(residual.at[:, my_lanes], res, local_sem.at[1])
    load_wv = pltpu.make_async_copy(experts, wv.at[0], local_sem.at[2])
    load_ow.start()
    load_res.start()
    load_wv.start()

    barrier = pltpu.get_barrier_semaphore()
    pl.semaphore_signal(barrier, inc=1, device_id=partner, device_id_type=pl.DeviceIdType.MESH)
    for dy, dx in PEERS:
        pl.semaphore_signal(barrier, inc=1, device_id={"tp": peer_of(dy, dx)}, device_id_type=pl.DeviceIdType.MESH)
    for k in range(1, EXP):
        pl.semaphore_signal(barrier, inc=1, device_id={"exp": lax.rem(z + k, EXP)}, device_id_type=pl.DeviceIdType.MESH)
    pl.semaphore_wait(barrier, 1 + len(PEERS) + EXP - 1)

    send_halo = remote(conv_in.at[pl.ds(TOKENS - 16, 16)], halo, ctx_send.at[0], ctx_recv.at[0], partner)

    @pl.when(core == 0)
    def _():
        send_halo.start()
        halo[...] = jnp.zeros_like(halo)

    ext[pl.ds(8, TOKENS), :] = conv_in[...].astype(F32)

    @pl.when(core == 1)
    def _():
        send_halo.wait_recv()

    ext[pl.ds(0, 8), :] = halo[...].astype(F32)[8:16]
    convolved = conv_b[...] + sum(conv_w[pl.ds(k, 1), :] * ext[pl.ds(5 + k, TOKENS), :] for k in range(4))
    xconv = silu(convolved).astype(BF16)

    part = dot(xconv, proj_w[...], ((1,), (1,))).reshape(TP, 8, RANK + 2 * STATE)
    psend[...] = part.astype(BF16)
    copies = []
    for i, (dy, dx) in enumerate(PEERS):
        peer = peer_of(dy, dx)
        c = remote(psend.at[peer], precv.at[i], p_send.at[i], p_recv.at[i], {"tp": peer})
        c.start()
        copies.append(c)

    expert = lax.broadcasted_iota(jnp.int32, (EXP, TOKENS), 0)
    hot = [(expert == ids[pl.ds(p, 1), :]).astype(F32) for p in range(2)]
    row = lax.broadcasted_iota(jnp.int32, (TOKENS, TOKENS), 0)
    col = lax.broadcasted_iota(jnp.int32, (TOKENS, TOKENS), 1)
    counts = dot((hot[0] + hot[1]).astype(BF16), (row < col).astype(BF16))
    slot = lax.broadcasted_iota(jnp.int32, (ROWS, TOKENS), 0).astype(F32)
    taken = [
        (slot == ids[pl.ds(p, 1), :].astype(F32) * CAP + jnp.sum(hot[p] * counts, axis=0, keepdims=True)).astype(F32)
        for p in range(2)
    ]
    chooser = (taken[0] + taken[1]).astype(BF16)
    blend = taken[0] * gates[pl.ds(0, 1), :] + taken[1] * gates[pl.ds(1, 1), :]
    blend_hi = blend.astype(BF16)
    blend_lo = (blend - blend_hi.astype(F32)).astype(BF16)
    xfloat = xconv.astype(F32)
    gate = silu(gate_in[...].astype(F32))

    total = psend[tp].astype(F32)
    for i, c in enumerate(copies):
        c.wait_recv()
        total = total + precv[i].astype(F32)
    for c in copies:
        c.wait_send()
    pall[tp] = total.astype(BF16)
    copies = []
    for i, (dy, dx) in enumerate(PEERS):
        c = remote(pall.at[tp], pall.at[tp], a_send.at[i], a_recv.at[i], {"tp": peer_of(dy, dx)})
        c.start()
        copies.append(c)
    for c in copies:
        c.wait_send()
    for c in copies:
        c.wait_recv()
    projected = pall[...].astype(F32).reshape(TOKENS, RANK + 2 * STATE)
    rank_part = projected[:, :RANK].astype(BF16)
    maps = projected[:, RANK:]

    eye = (
        lax.broadcasted_iota(jnp.int32, (2 * STATE, 2 * STATE), 0) == lax.broadcasted_iota(jnp.int32, (2 * STATE, 2 * STATE), 1)
    ).astype(F32)
    spread = (maps[:, None, :] * eye[None]).reshape(TOKENS * 2 * STATE, 2 * STATE).astype(BF16)
    mb[...] = dot(spread, jnp.ones((2 * STATE, 128), BF16)).reshape(TOKENS, 2 * STATE, 128)

    raw = dot(rank_part, step_w[...]) + step_b[...]
    step_sizes = jnp.maximum(raw, 0.0) + jnp.log1p(jnp.exp(-jnp.abs(raw)))
    steps[...] = step_sizes
    driven[...] = step_sizes * xfloat
    decay = -jnp.exp(decay_log[...])
    send_state = remote(hend, hstart, ctx_send.at[1], ctx_recv.at[1], partner)

    @pl.when(core == 0)
    def _():
        hstart[...] = jnp.zeros_like(hstart)

    @pl.when(core == 1)
    def _():
        send_state.wait_recv()

    def scan_block(block, h):
        for i in range(8):
            t = block * 8 + i
            m = mb[t]
            in_map = jnp.concatenate([m[:STATE], m[:STATE]], axis=1)
            out_map = jnp.concatenate([m[STATE:], m[STATE:]], axis=1)
            h = jnp.exp(steps[pl.ds(t, 1), :] * decay) * h + driven[pl.ds(t, 1), :] * in_map
            ys[pl.ds(t, 1), :] = jnp.sum(out_map * h, axis=0, keepdims=True)
        return h

    hend[...] = lax.fori_loop(0, TOKENS // 8, scan_block, hstart[...])

    @pl.when(core == 0)
    def _():
        send_state.start()

    send_w = remote(experts, wv.at[1], ctx_send.at[2], ctx_recv.at[2], partner)
    send_w.start()
    gated = ((ys[...] + skip[...] * xfloat) * gate).astype(BF16)

    load_ow.wait()
    load_res.wait()
    copies = []
    i = 0
    for dy in (2, 1, 3, 0):
        yy = lax.rem(my_y + dy, SIDE)
        piece = dot(gated, ow[:, pl.ds(pl.multiple_of(yy * 512, 512), 512)])
        for j in range(SIDE):
            osend[yy * SIDE + j] = piece[:, j * 128 : (j + 1) * 128].astype(BF16)
        for dx in (2, 1, 3, 0):
            if (dy, dx) == (0, 0):
                continue
            peer = peer_of(dy, dx)
            c = remote(osend.at[peer], orecv.at[i], o_send.at[i], o_recv.at[i], {"tp": peer})
            c.start()
            copies.append(c)
            i += 1
    mixed = osend[tp].astype(F32)
    for i, c in enumerate(copies):
        c.wait_recv()
        mixed = mixed + orecv[i].astype(F32)
    stream = (res[...].astype(F32) + mixed).astype(BF16)

    chosen = dot(chooser, stream).astype(BF16).reshape(EXP, CAP, 128)
    picked[...] = chosen
    zcopies = [None] * EXP
    for pos, k in enumerate(NEAR):
        if k:
            dest = lax.rem(z + EXP - k, EXP)
            c = remote(picked.at[dest], xs.at[pl.ds(pos * CAP, CAP), my_lanes], z_send.at[pos], z_recv.at[pos], {"exp": dest})
            c.start()
            zcopies[pos] = c
    keep = pltpu.make_async_copy(picked.at[z], xs.at[pl.ds(0, CAP), my_lanes], local_sem.at[3])
    keep.start()
    keep.wait()
    gcopies = []
    for g in range(2):
        for pos in range(g * 4, g * 4 + 4):
            if zcopies[pos] is not None:
                zcopies[pos].wait_recv()
        block = xs.at[pl.ds(g * GROUP, GROUP), my_lanes]
        mine = []
        for i, (dy, dx) in enumerate(PEERS):
            c = remote(block, block, g_send.at[g, i], g_recv.at[g, i], {"tp": peer_of(dy, dx)})
            c.start()
            mine.append(c)
        gcopies.append(mine)
    for c in copies:
        c.wait_send()
    load_wv.wait()

    rcopies = []
    for g in range(2):
        for c in gcopies[g]:
            c.wait_recv()

        def norm_rows(r, _, g=g):
            at = pl.ds(pl.multiple_of(g * GROUP + r * 16, 16), 16)
            rows = xs[at, :].astype(F32)
            scale = lax.rsqrt(jnp.mean(rows * rows, axis=1, keepdims=True) + 1e-06)
            xn[pl.ds(pl.multiple_of(r * 16, 16), 16), :] = (rows * scale * gain[...]).astype(BF16)
            return 0

        lax.fori_loop(0, GROUP // 16, norm_rows, 0)
        if g == 0:
            send_w.wait_recv()

        def up_half(w, _):
            gate_part = dot(xn[...], wv[w, 0], ((1,), (1,)))
            up_part = dot(xn[...], wv[w, 1], ((1,), (1,)))
            hid[w] = (silu(gate_part) * up_part).astype(BF16)
            return 0

        lax.fori_loop(0, 2, up_half, 0)
        mine = []
        i = 0
        for dy in (2, 1, 3, 0):
            yy = lax.rem(my_y + dy, SIDE)
            down = pl.ds(pl.multiple_of(yy * 512, 512), 512)
            piece = dot(hid[0], wv[0, 2, :, down]) + dot(hid[1], wv[1, 2, :, down])
            for j in range(SIDE):
                rsend[g, yy * SIDE + j] = piece[:, j * 128 : (j + 1) * 128].astype(BF16)
            for dx in (2, 1, 3, 0):
                if (dy, dx) == (0, 0):
                    continue
                peer = peer_of(dy, dx)
                c = remote(rsend.at[g, peer], rrecv.at[g, i], r_send.at[g, i], r_recv.at[g, i], {"tp": peer})
                c.start()
                mine.append(c)
                i += 1
        rcopies.append(mine)

    bcopies = []
    for g in range(2):
        total = rsend[g, tp].astype(F32)
        for i, c in enumerate(rcopies[g]):
            c.wait_recv()
            total = total + rrecv[g, i].astype(F32)
        ret_send[pl.ds(g * GROUP, GROUP), :] = total.astype(BF16)
        for pos in range(g * 4, g * 4 + 4):
            k = NEAR[pos]
            src = ret_send.at[pl.ds(pos * CAP, CAP)]
            dst = ret.at[pl.ds(pl.multiple_of(z * CAP, CAP), CAP)]
            if k:
                c = remote(src, dst, b_send.at[pos], b_recv.at[pos], {"exp": lax.rem(z + k, EXP)})
            else:
                c = pltpu.make_async_copy(src, dst, local_sem.at[4])
            c.start()
            bcopies.append(c)
    for pos, c in enumerate(bcopies):
        if NEAR[pos]:
            c.wait_recv()
        else:
            c.wait()
    back = ret[...]
    moe = dot(blend_hi, back, ((0,), (0,))) + dot(blend_lo, back, ((0,), (0,)))
    out[...] = (stream.astype(F32) + moe).astype(BF16)

    @pl.when(core == 0)
    def _():
        send_halo.wait_send()
        send_state.wait_send()

    send_w.wait_send()
    for c in zcopies[1:] + gcopies[0] + gcopies[1] + rcopies[0] + rcopies[1]:
        c.wait_send()
    for pos, c in enumerate(bcopies):
        if NEAR[pos]:
            c.wait_send()


def body(
    conv_in, gate_in, residual, conv_weight, conv_bias, proj_weight, step_weight, step_bias, decay_log, skip_gain, out_weight, norm_gain,
    expert_ids, route_gates, expert_weight,
):
    vmem, hbm = pl.BlockSpec(memory_space=pltpu.VMEM), pl.BlockSpec(memory_space=pl.ANY)
    dma, n = pltpu.SemaphoreType.DMA, len(PEERS)
    wide = RANK + 2 * STATE
    result = pl.pallas_call(
        kernel,
        out_shape=jax.ShapeDtypeStruct((TOKENS, 128), BF16),
        in_specs=[vmem, vmem, hbm, vmem, vmem, vmem, vmem, vmem, vmem, vmem, hbm, vmem, vmem, vmem, hbm],
        out_specs=vmem,
        scratch_shapes=[
            pltpu.VMEM((16, CHANNELS), BF16),
            pltpu.VMEM((TOKENS + 8, CHANNELS), F32),
            pltpu.VMEM((TP, 8, wide), BF16),
            pltpu.VMEM((n, 8, wide), BF16),
            pltpu.VMEM((TP, 8, wide), BF16),
            pltpu.VMEM((TOKENS, 2 * STATE, 128), F32),
            pltpu.VMEM((TOKENS, CHANNELS), F32),
            pltpu.VMEM((TOKENS, CHANNELS), F32),
            pltpu.VMEM((TOKENS, CHANNELS), F32),
            pltpu.VMEM((STATE, CHANNELS), F32),
            pltpu.VMEM((STATE, CHANNELS), F32),
            pltpu.VMEM((CHANNELS, D), BF16),
            pltpu.VMEM((TOKENS, 128), BF16),
            pltpu.VMEM((TP, TOKENS, 128), BF16),
            pltpu.VMEM((n, TOKENS, 128), BF16),
            pltpu.VMEM((EXP, CAP, 128), BF16),
            pltpu.VMEM((ROWS, D), BF16),
            pltpu.VMEM((GROUP, D), BF16),
            pltpu.VMEM((2, 3, HIDDEN, D), BF16),
            pltpu.VMEM((2, GROUP, HIDDEN), BF16),
            pltpu.VMEM((2, TP, GROUP, 128), BF16),
            pltpu.VMEM((2, n, GROUP, 128), BF16),
            pltpu.VMEM((ROWS, 128), BF16),
            pltpu.VMEM((ROWS, 128), BF16),
            dma((5,)), dma((3,)), dma((3,)),
            dma((n,)), dma((n,)), dma((n,)), dma((n,)), dma((n,)), dma((n,)),
            dma((EXP,)), dma((EXP,)),
            dma((2, n)), dma((2, n)), dma((2, n)), dma((2, n)),
            dma((EXP,)), dma((EXP,)),
        ],
        compiler_params=pltpu.CompilerParams(collective_id=0, has_side_effects=True, vmem_limit_bytes=60 << 20),
        name="mixer_experts",
    )(
        conv_in[0], gate_in[0], residual[0], conv_weight, conv_bias[None], proj_weight.T, step_weight, step_bias[None], decay_log,
        skip_gain[None], out_weight, norm_gain[None], expert_ids[0].T, route_gates[0].T,
        jnp.swapaxes(expert_weight[0], 1, 2),
    )
    return result[None]


def solution(mesh):
    placed = (
        P("exp", "ctx", "tp"),
        P("exp", "ctx", "tp"),
        P("exp", "ctx", None),
        P(None, "tp"),
        P("tp"),
        P("tp", None),
        P(None, "tp"),
        P("tp"),
        P(None, "tp"),
        P("tp"),
        P("tp", None),
        P(),
        P("exp", "ctx", None),
        P("exp", "ctx", None),
        P("exp", None, None, ("ctx", "tp")),
    )
    return jax.shard_map(body, mesh=mesh, in_specs=placed, out_specs=P("exp", "ctx", "tp"), check_vma=False)
```

```python
import functools

import jax
import jax.numpy as jnp
from jax import lax
from jax.experimental import pallas as pl
from jax.experimental.pallas import tpu as pltpu
from jax.sharding import PartitionSpec as P

F32, BF16 = jnp.float32, jnp.bfloat16
D = 2048
STATE = 16
RANK = 256
CAP = 64
TOKENS = 128
CHANNELS = 256
HIDDEN = 448
SIDE = 4
TP = 16
EXP = 8
ROWS = EXP * CAP
GROUP = ROWS // 2
NEAR = (0, 1, 7, 2, 6, 3, 5, 4)
PEERS = [(dy, dx) for dy in (2, 1, 3, 0) for dx in (2, 1, 3, 0) if (dy, dx) != (0, 0)]


def dot(a, b, dims=((1,), (0,))):
    return lax.dot_general(a, b, (dims, ((), ())), preferred_element_type=F32)


def silu(v):
    return v * jax.nn.sigmoid(v)


def kernel(
    conv_in, gate_in, residual, conv_w, conv_b, proj_w, step_w, step_b, decay_log, skip, out_w, gain, ids, gates, experts,
    out,
    halo, ext, psend, precv, pall, mb, steps, driven, ys, hend, hstart, ow, res, osend, orecv, picked, xs, xn, wv, hid, rsend, one, half_sum, two,
    ret_send, ret,
    local_sem, ctx_send, ctx_recv, p_send, p_recv, a_send, a_recv, o_send, o_recv, z_send, z_recv, g_send, g_recv, r_send, r_recv, q_send, q_recv, b_send, b_recv,
):
    core, z, tp = lax.axis_index("ctx"), lax.axis_index("exp"), lax.axis_index("tp")
    my_y, my_x = tp // SIDE, lax.rem(tp, SIDE)
    partner = {"ctx": 1 - core}

    def peer_of(dy, dx):
        return lax.rem(my_y + dy, SIDE) * SIDE + lax.rem(my_x + dx, SIDE)

    def remote(src, dst, ss, rs, device):
        return pltpu.make_async_remote_copy(
            src_ref=src, dst_ref=dst, send_sem=ss, recv_sem=rs, device_id=device, device_id_type=pl.DeviceIdType.MESH
        )

    my_lanes = pl.ds(pl.multiple_of(tp * 128, 128), 128)
    load_ow = pltpu.make_async_copy(out_w, ow, local_sem.at[0])
    load_res = pltpu.make_async_copy(residual.at[:, my_lanes], res, local_sem.at[1])
    load_wv = pltpu.make_async_copy(experts, wv.at[0], local_sem.at[2])
    load_ow.start()
    load_res.start()
    load_wv.start()

    barrier = pltpu.get_barrier_semaphore()
    pl.semaphore_signal(barrier, inc=1, device_id=partner, device_id_type=pl.DeviceIdType.MESH)
    for dy, dx in PEERS:
        pl.semaphore_signal(barrier, inc=1, device_id={"tp": peer_of(dy, dx)}, device_id_type=pl.DeviceIdType.MESH)
    for k in range(1, EXP):
        pl.semaphore_signal(barrier, inc=1, device_id={"exp": lax.rem(z + k, EXP)}, device_id_type=pl.DeviceIdType.MESH)
    pl.semaphore_wait(barrier, 1 + len(PEERS) + EXP - 1)

    send_halo = remote(conv_in.at[pl.ds(TOKENS - 16, 16)], halo, ctx_send.at[0], ctx_recv.at[0], partner)

    @pl.when(core == 0)
    def _():
        send_halo.start()
        halo[...] = jnp.zeros_like(halo)

    ext[pl.ds(8, TOKENS), :] = conv_in[...].astype(F32)

    @pl.when(core == 1)
    def _():
        send_halo.wait_recv()

    ext[pl.ds(0, 8), :] = halo[...].astype(F32)[8:16]
    convolved = conv_b[...] + sum(conv_w[pl.ds(k, 1), :] * ext[pl.ds(5 + k, TOKENS), :] for k in range(4))
    xconv = silu(convolved).astype(BF16)

    part = dot(xconv, proj_w[...], ((1,), (1,))).reshape(TP, 8, RANK + 2 * STATE)
    psend[...] = part.astype(BF16)
    copies = []
    for i, (dy, dx) in enumerate(PEERS):
        peer = peer_of(dy, dx)
        c = remote(psend.at[peer], precv.at[i], p_send.at[i], p_recv.at[i], {"tp": peer})
        c.start()
        copies.append(c)

    expert = lax.broadcasted_iota(jnp.int32, (EXP, TOKENS), 0)
    hot = [(expert == ids[pl.ds(p, 1), :]).astype(F32) for p in range(2)]
    row = lax.broadcasted_iota(jnp.int32, (TOKENS, TOKENS), 0)
    col = lax.broadcasted_iota(jnp.int32, (TOKENS, TOKENS), 1)
    counts = dot((hot[0] + hot[1]).astype(BF16), (row < col).astype(BF16))
    slot = lax.broadcasted_iota(jnp.int32, (ROWS, TOKENS), 0).astype(F32)
    taken = [
        (slot == ids[pl.ds(p, 1), :].astype(F32) * CAP + jnp.sum(hot[p] * counts, axis=0, keepdims=True)).astype(F32)
        for p in range(2)
    ]
    chooser = (taken[0] + taken[1]).astype(BF16)
    blend = taken[0] * gates[pl.ds(0, 1), :] + taken[1] * gates[pl.ds(1, 1), :]
    blend_hi = blend.astype(BF16)
    blend_lo = (blend - blend_hi.astype(F32)).astype(BF16)
    xfloat = xconv.astype(F32)
    gate = silu(gate_in[...].astype(F32))

    total = psend[tp].astype(F32)
    for i, c in enumerate(copies):
        c.wait_recv()
        total = total + precv[i].astype(F32)
    for c in copies:
        c.wait_send()
    pall[tp] = total.astype(BF16)
    copies = []
    for i, (dy, dx) in enumerate(PEERS):
        c = remote(pall.at[tp], pall.at[tp], a_send.at[i], a_recv.at[i], {"tp": peer_of(dy, dx)})
        c.start()
        copies.append(c)
    for c in copies:
        c.wait_send()
    for c in copies:
        c.wait_recv()
    projected = pall[...].astype(F32).reshape(TOKENS, RANK + 2 * STATE)
    rank_part = projected[:, :RANK].astype(BF16)
    maps = projected[:, RANK:]

    eye = (
        lax.broadcasted_iota(jnp.int32, (2 * STATE, 2 * STATE), 0) == lax.broadcasted_iota(jnp.int32, (2 * STATE, 2 * STATE), 1)
    ).astype(F32)
    spread = (maps[:, None, :] * eye[None]).reshape(TOKENS * 2 * STATE, 2 * STATE).astype(BF16)
    mb[...] = dot(spread, jnp.ones((2 * STATE, 128), BF16)).reshape(TOKENS, 2 * STATE, 128)

    raw = dot(rank_part, step_w[...]) + step_b[...]
    step_sizes = jnp.maximum(raw, 0.0) + jnp.log1p(jnp.exp(-jnp.abs(raw)))
    steps[...] = step_sizes
    driven[...] = step_sizes * xfloat
    decay = -jnp.exp(decay_log[...])
    send_state = remote(hend, hstart, ctx_send.at[1], ctx_recv.at[1], partner)

    @pl.when(core == 0)
    def _():
        hstart[...] = jnp.zeros_like(hstart)

    @pl.when(core == 1)
    def _():
        send_state.wait_recv()

    def scan_block(block, h):
        for i in range(8):
            t = block * 8 + i
            m = mb[t]
            in_map = jnp.concatenate([m[:STATE], m[:STATE]], axis=1)
            out_map = jnp.concatenate([m[STATE:], m[STATE:]], axis=1)
            h = jnp.exp(steps[pl.ds(t, 1), :] * decay) * h + driven[pl.ds(t, 1), :] * in_map
            ys[pl.ds(t, 1), :] = jnp.sum(out_map * h, axis=0, keepdims=True)
        return h

    hend[...] = lax.fori_loop(0, TOKENS // 8, scan_block, hstart[...])

    @pl.when(core == 0)
    def _():
        send_state.start()

    send_w = remote(experts, wv.at[1], ctx_send.at[2], ctx_recv.at[2], partner)
    send_w.start()
    gated = ((ys[...] + skip[...] * xfloat) * gate).astype(BF16)

    load_ow.wait()
    load_res.wait()
    copies = []
    i = 0
    for dy in (2, 1, 3, 0):
        yy = lax.rem(my_y + dy, SIDE)
        piece = dot(gated, ow[:, pl.ds(pl.multiple_of(yy * 512, 512), 512)])
        for j in range(SIDE):
            osend[yy * SIDE + j] = piece[:, j * 128 : (j + 1) * 128].astype(BF16)
        for dx in (2, 1, 3, 0):
            if (dy, dx) == (0, 0):
                continue
            peer = peer_of(dy, dx)
            c = remote(osend.at[peer], orecv.at[i], o_send.at[i], o_recv.at[i], {"tp": peer})
            c.start()
            copies.append(c)
            i += 1
    mixed = osend[tp].astype(F32)
    for i, c in enumerate(copies):
        c.wait_recv()
        mixed = mixed + orecv[i].astype(F32)
    stream = (res[...].astype(F32) + mixed).astype(BF16)

    chosen = dot(chooser, stream).astype(BF16).reshape(EXP, CAP, 128)
    picked[...] = chosen
    zcopies = [None] * EXP
    for pos, k in enumerate(NEAR):
        if k:
            dest = lax.rem(z + EXP - k, EXP)
            c = remote(picked.at[dest], xs.at[pl.ds(pos * CAP, CAP), my_lanes], z_send.at[pos], z_recv.at[pos], {"exp": dest})
            c.start()
            zcopies[pos] = c
    keep = pltpu.make_async_copy(picked.at[z], xs.at[pl.ds(0, CAP), my_lanes], local_sem.at[3])
    keep.start()
    keep.wait()
    def chip(h, du, dv):
        return peer_of((dv if h == 0 else du) % SIDE, (du if h == 0 else dv) % SIDE)

    sent = []
    FAR = (2, 1, 3)

    def gather(g, h):
        rows = pl.ds(g * GROUP + h * 128, 128)

        def part_of(du, dv):
            return xs.at[rows, pl.ds(pl.multiple_of(chip(h, du, dv) * 128, 128), 128)]

        def put(m, to, origin):
            ref = part_of(*origin)
            c = remote(ref, ref, g_send.at[g, h, m], g_recv.at[g, h, m], {"tp": chip(h, *to)})
            c.start()
            sent.append(c)

        def got(m, origin):
            ref = part_of(*origin)
            remote(ref, ref, g_send.at[g, h, m], g_recv.at[g, h, m], {"tp": tp}).wait_recv()

        for pos in range(g * 4 + h * 2, g * 4 + h * 2 + 2):
            if zcopies[pos] is not None:
                zcopies[pos].wait_recv()
        for d in FAR:
            put(d - 1, (d, 0), (0, 0))
        for d in FAR:
            put(3 + d - 1, (0, d), (0, 0))
        yield
        for u in (1, 3, 2):
            got(SIDE - u - 1, (u, 0))
            for d in FAR:
                put(3 + 3 * u + d - 1, (0, d), (u, 0))
            yield
        for u in range(SIDE):
            for d in FAR:
                got(3 + 3 * u + d - 1, (u, SIDE - d))
        yield

    def scatter(g, h):
        my_a, my_b = (my_y, my_x) if h == 0 else (my_x, my_y)

        def near(at, d):
            return lax.rem(at + d, SIDE)

        def tiles(d, q):
            rows = pl.ds(h * 128 + q * 64, 64)
            return rsend.at[g, near(my_a, d), :, rows, :] if h == 0 else rsend.at[g, :, near(my_a, d), rows, :]

        def lane(d, q):
            return half_sum.at[g, h, near(my_b, d), pl.ds(q * 64, 64), :]

        def arrived(buf, ss, rs, q, d):
            ref = buf.at[g, h, q, d - 1]
            remote(ref, ref, ss.at[g, h, q, d - 1], rs.at[g, h, q, d - 1], {"tp": tp}).wait_recv()
            return ref[...].astype(F32)

        for d in FAR:
            for q in range(2):
                c = remote(tiles(d, q), one.at[g, h, q, d - 1], r_send.at[g, h, q, d - 1], r_recv.at[g, h, q, d - 1], {"tp": chip(h, 0, d)})
                c.start()
                sent.append(c)
            yield
        for q in range(2):
            total = tiles(0, q)[...].astype(F32)
            for d in range(1, SIDE):
                total = total + arrived(one, r_send, r_recv, q, d)
            half_sum[g, h, :, pl.ds(q * 64, 64), :] = total.astype(BF16)
            for d in FAR:
                c = remote(lane(d, q), two.at[g, h, q, d - 1], q_send.at[g, h, q, d - 1], q_recv.at[g, h, q, d - 1], {"tp": chip(h, d, 0)})
                c.start()
                sent.append(c)
            yield
        for q in range(2):
            pos = g * 4 + h * 2 + q
            total = lane(0, q)[...].astype(F32)
            for d in range(1, SIDE):
                total = total + arrived(two, q_send, q_recv, q, d)
            rows = pl.ds(pos * CAP, CAP)
            ret_send[rows, :] = total.astype(BF16)
            dst = ret.at[pl.ds(pl.multiple_of(z * CAP, CAP), CAP)]
            k = NEAR[pos]
            if k:
                c = remote(ret_send.at[rows], dst, b_send.at[pos], b_recv.at[pos], {"exp": lax.rem(z + k, EXP)})
            else:
                c = pltpu.make_async_copy(ret_send.at[rows], dst, local_sem.at[4])
            c.start()
            bcopies[pos] = c
            yield

    bcopies = [None] * EXP
    gathers = [[gather(g, h) for h in range(2)] for g in range(2)]
    scatters = [[scatter(g, h) for h in range(2)] for g in range(2)]

    def step(pair):
        for one_of in pair:
            next(one_of)

    step(gathers[0])
    step(gathers[0])
    step(gathers[0])
    step(gathers[0])
    step(gathers[1])
    for c in copies:
        c.wait_send()
    load_wv.wait()
    step(gathers[0])

    def normalize(g):
        def norm_rows(r, _):
            rows = xs[pl.ds(pl.multiple_of(g * GROUP + r * 64, 64), 64), :].astype(F32)
            scale = lax.rsqrt(jnp.mean(rows * rows, axis=1, keepdims=True) + 1e-06)
            xn[pl.ds(pl.multiple_of(r * 64, 64), 64), :] = (rows * scale * gain[...]).astype(BF16)
            return 0

        lax.fori_loop(0, GROUP // 64, norm_rows, 0)

    def up(w):
        gate_part = dot(xn[...], wv[w, 0], ((1,), (1,)))
        up_part = dot(xn[...], wv[w, 1], ((1,), (1,)))
        hid[w] = (silu(gate_part) * up_part).astype(BF16)

    def down(g, dy):
        yy = lax.rem(my_y + dy, SIDE)
        cols = pl.ds(pl.multiple_of(yy * 512, 512), 512)
        piece = dot(hid[0], wv[0, 2, :, cols]) + dot(hid[1], wv[1, 2, :, cols])
        for j in range(SIDE):
            rsend[g, yy, j] = piece[:, j * 128 : (j + 1) * 128].astype(BF16)

    def all_down(g):
        for dy in (2, 1, 3, 0):
            down(g, dy)
            if dy:
                next(scatters[g][0])
        for _ in range(3):
            next(scatters[g][1])

    normalize(0)
    step(gathers[1])
    step(gathers[1])
    send_w.wait_recv()
    up(0)
    step(gathers[1])
    up(1)
    all_down(0)
    step(gathers[1])
    normalize(1)
    up(0)
    up(1)
    all_down(1)
    step(scatters[0])
    step(scatters[0])
    step(scatters[1])
    step(scatters[0])
    step(scatters[0])
    step(scatters[1])
    step(scatters[1])
    step(scatters[1])
    for pos, c in enumerate(bcopies):
        if NEAR[pos]:
            c.wait_recv()
        else:
            c.wait()
    back = ret[...]
    moe = dot(blend_hi, back, ((0,), (0,))) + dot(blend_lo, back, ((0,), (0,)))
    out[...] = (stream.astype(F32) + moe).astype(BF16)

    @pl.when(core == 0)
    def _():
        send_halo.wait_send()
        send_state.wait_send()

    send_w.wait_send()
    for c in zcopies[1:] + sent:
        c.wait_send()
    for pos, c in enumerate(bcopies):
        if NEAR[pos]:
            c.wait_send()


def body(
    conv_in, gate_in, residual, conv_weight, conv_bias, proj_weight, step_weight, step_bias, decay_log, skip_gain, out_weight, norm_gain,
    expert_ids, route_gates, expert_weight,
):
    vmem, hbm = pl.BlockSpec(memory_space=pltpu.VMEM), pl.BlockSpec(memory_space=pl.ANY)
    dma, n = pltpu.SemaphoreType.DMA, len(PEERS)
    wide = RANK + 2 * STATE
    result = pl.pallas_call(
        kernel,
        out_shape=jax.ShapeDtypeStruct((TOKENS, 128), BF16),
        in_specs=[vmem, vmem, hbm, vmem, vmem, vmem, vmem, vmem, vmem, vmem, hbm, vmem, vmem, vmem, hbm],
        out_specs=vmem,
        scratch_shapes=[
            pltpu.VMEM((16, CHANNELS), BF16),
            pltpu.VMEM((TOKENS + 8, CHANNELS), F32),
            pltpu.VMEM((TP, 8, wide), BF16),
            pltpu.VMEM((n, 8, wide), BF16),
            pltpu.VMEM((TP, 8, wide), BF16),
            pltpu.VMEM((TOKENS, 2 * STATE, 128), F32),
            pltpu.VMEM((TOKENS, CHANNELS), F32),
            pltpu.VMEM((TOKENS, CHANNELS), F32),
            pltpu.VMEM((TOKENS, CHANNELS), F32),
            pltpu.VMEM((STATE, CHANNELS), F32),
            pltpu.VMEM((STATE, CHANNELS), F32),
            pltpu.VMEM((CHANNELS, D), BF16),
            pltpu.VMEM((TOKENS, 128), BF16),
            pltpu.VMEM((TP, TOKENS, 128), BF16),
            pltpu.VMEM((n, TOKENS, 128), BF16),
            pltpu.VMEM((EXP, CAP, 128), BF16),
            pltpu.VMEM((ROWS, D), BF16),
            pltpu.VMEM((GROUP, D), BF16),
            pltpu.VMEM((2, 3, HIDDEN, D), BF16),
            pltpu.VMEM((2, GROUP, HIDDEN), BF16),
            pltpu.VMEM((2, SIDE, SIDE, GROUP, 128), BF16),
            pltpu.VMEM((2, 2, 2, 3, SIDE, 64, 128), BF16),
            pltpu.VMEM((2, 2, SIDE, 128, 128), BF16),
            pltpu.VMEM((2, 2, 2, 3, 64, 128), BF16),
            pltpu.VMEM((ROWS, 128), BF16),
            pltpu.VMEM((ROWS, 128), BF16),
            dma((5,)), dma((3,)), dma((3,)),
            dma((n,)), dma((n,)), dma((n,)), dma((n,)), dma((n,)), dma((n,)),
            dma((EXP,)), dma((EXP,)),
            dma((2, 2, 15)), dma((2, 2, 15)),
            dma((2, 2, 2, 3)), dma((2, 2, 2, 3)), dma((2, 2, 2, 3)), dma((2, 2, 2, 3)),
            dma((EXP,)), dma((EXP,)),
        ],
        compiler_params=pltpu.CompilerParams(collective_id=0, has_side_effects=True, vmem_limit_bytes=60 << 20),
        name="mixer_experts",
    )(
        conv_in[0], gate_in[0], residual[0], conv_weight, conv_bias[None], proj_weight.T, step_weight, step_bias[None], decay_log,
        skip_gain[None], out_weight, norm_gain[None], expert_ids[0].T, route_gates[0].T,
        jnp.swapaxes(expert_weight[0], 1, 2),
    )
    return result[None]


def solution(mesh):
    placed = (
        P("exp", "ctx", "tp"),
        P("exp", "ctx", "tp"),
        P("exp", "ctx", None),
        P(None, "tp"),
        P("tp"),
        P("tp", None),
        P(None, "tp"),
        P("tp"),
        P(None, "tp"),
        P("tp"),
        P("tp", None),
        P(),
        P("exp", "ctx", None),
        P("exp", "ctx", None),
        P("exp", None, None, ("ctx", "tp")),
    )
    return jax.shard_map(body, mesh=mesh, in_specs=placed, out_specs=P("exp", "ctx", "tp"), check_vma=False)
```

```python
import functools

import jax
import jax.numpy as jnp
from jax import lax
from jax.experimental import pallas as pl
from jax.experimental.pallas import tpu as pltpu
from jax.sharding import PartitionSpec as P

F32, BF16 = jnp.float32, jnp.bfloat16
D = 2048
STATE = 16
RANK = 256
CAP = 64
TOKENS = 128
CHANNELS = 256
HIDDEN = 448
SIDE = 4
TP = 16
EXP = 8
ROWS = EXP * CAP
GROUP = ROWS // 2
NEAR = (0, 1, 7, 2, 4, 6, 3, 5)
UNITS = ((0, 32, 0), (32, 32, 1), (64, 64, 0), (128, 64, 1), (192, 32, 0), (224, 32, 1), (256, 128, 0), (384, 128, 1))
SPREAD = (2, 3, 4, 5)
PEERS = [(dy, dx) for dy in (2, 1, 3, 0) for dx in (2, 1, 3, 0) if (dy, dx) != (0, 0)]


def dot(a, b, dims=((1,), (0,))):
    return lax.dot_general(a, b, (dims, ((), ())), preferred_element_type=F32)


def silu(v):
    return v * jax.nn.sigmoid(v)


def kernel(
    conv_hbm, gate_hbm, residual, conv_w_hbm, conv_b_hbm, proj_w_hbm, step_w_hbm, step_b_hbm, decay_hbm, skip_hbm, out_w, gain_hbm, ids_hbm, gates_hbm, experts,
    out,
    conv_in, gate_in, conv_w, conv_b, proj_w, step_w, step_b, decay_log, skip, gain, ids, gates, xc,
    halo, ext, psend, precv, pall, mb, steps, driven, ys, hend, hstart, ow, res, osend, orecv, ohalf, orecv2, picked, xs, xn, wv, hid, rsend, one, half_sum, two,
    ret_send, ret,
    in_sem, local_sem, ctx_send, ctx_recv, p_send, p_recv, a_send, a_recv, o_send, o_recv, z_send, z_recv, g_send, g_recv, r_send, r_recv, q_send, q_recv, b_send, b_recv,
):
    core, z, tp = lax.axis_index("ctx"), lax.axis_index("exp"), lax.axis_index("tp")
    my_y, my_x = tp // SIDE, lax.rem(tp, SIDE)
    partner = {"ctx": 1 - core}

    def peer_of(dy, dx):
        return lax.rem(my_y + dy, SIDE) * SIDE + lax.rem(my_x + dx, SIDE)

    def chip(h, du, dv):
        return peer_of((dv if h == 0 else du) % SIDE, (du if h == 0 else dv) % SIDE)

    def remote(src, dst, ss, rs, device):
        return pltpu.make_async_remote_copy(
            src_ref=src, dst_ref=dst, send_sem=ss, recv_sem=rs, device_id=device, device_id_type=pl.DeviceIdType.MESH
        )

    my_lanes = pl.ds(pl.multiple_of(tp * 128, 128), 128)
    barrier = pltpu.get_barrier_semaphore()
    for dy, dx in PEERS:
        pl.semaphore_signal(barrier, inc=1, device_id={"tp": peer_of(dy, dx)}, device_id_type=pl.DeviceIdType.MESH)
    for k in range(1, EXP):
        pl.semaphore_signal(barrier, inc=1, device_id={"exp": lax.rem(z + k, EXP)}, device_id_type=pl.DeviceIdType.MESH)
    for k, h in ((1, 0), (7, 1), (2, 0), (2, 1)):
        for d in range(1, SIDE):
            device = {"exp": lax.rem(z + k, EXP), "tp": chip(h, d, 0)}
            pl.semaphore_signal(barrier, inc=1, device_id=device, device_id_type=pl.DeviceIdType.MESH)
    pl.semaphore_signal(barrier, inc=1, device_id=partner, device_id_type=pl.DeviceIdType.MESH)
    loads = [
        pltpu.make_async_copy(src, dst, in_sem.at[i])
        for i, (src, dst) in enumerate(
            (
                (conv_hbm, conv_in), (conv_w_hbm, conv_w), (conv_b_hbm, conv_b), (proj_w_hbm, proj_w), (ids_hbm, ids), (gates_hbm, gates),
                (gate_hbm, gate_in), (step_w_hbm, step_w), (step_b_hbm, step_b), (decay_hbm, decay_log), (skip_hbm, skip), (gain_hbm, gain),
            )
        )
    ]
    load_ow = pltpu.make_async_copy(out_w, ow, local_sem.at[0])
    load_res = pltpu.make_async_copy(residual.at[:, my_lanes], res, local_sem.at[1])
    load_wv = pltpu.make_async_copy(experts, wv.at[0], local_sem.at[2])
    for c in loads + [load_ow, load_res, load_wv]:
        c.start()

    def convolve(count):
        convolved = conv_b[...] + sum(conv_w[pl.ds(k, 1), :] * ext[pl.ds(5 + k, count), :] for k in range(4))
        return silu(convolved).astype(BF16)

    def project(rows):
        count = rows.shape[0]
        return dot(rows, proj_w[...], ((1,), (1,))).reshape(count // 8, 8, RANK + 2 * STATE).astype(BF16)

    for c in loads[:4]:
        c.wait()
    ext[pl.ds(0, 8), :] = jnp.zeros((8, CHANNELS), F32)
    ext[pl.ds(8, TOKENS), :] = conv_in[...].astype(F32)
    xc[...] = convolve(TOKENS)
    psend[...] = project(xc[...])
    pl.semaphore_wait(barrier, 1 + len(PEERS) + EXP - 1 + 12)
    send_halo = remote(conv_hbm.at[pl.ds(TOKENS - 16, 16)], halo, ctx_send.at[0], ctx_recv.at[0], partner)

    @pl.when(core == 0)
    def _():
        send_halo.start()

    @pl.when(core == 1)
    def _():
        send_halo.wait_recv()
        ext[pl.ds(0, 8), :] = halo[...].astype(F32)[8:16]
        xc[pl.ds(0, 16), :] = convolve(16)
        psend[pl.ds(0, 2)] = project(xc[pl.ds(0, 16), :])

    copies = []
    for i, (dy, dx) in enumerate(PEERS):
        peer = peer_of(dy, dx)
        c = remote(psend.at[peer], precv.at[i], p_send.at[i], p_recv.at[i], {"tp": peer})
        c.start()
        copies.append(c)

    for c in loads[4:]:
        c.wait()
    expert = lax.broadcasted_iota(jnp.int32, (EXP, TOKENS), 0)
    hot = [(expert == ids[pl.ds(p, 1), :]).astype(F32) for p in range(2)]
    row = lax.broadcasted_iota(jnp.int32, (TOKENS, TOKENS), 0)
    col = lax.broadcasted_iota(jnp.int32, (TOKENS, TOKENS), 1)
    counts = dot((hot[0] + hot[1]).astype(BF16), (row < col).astype(BF16))
    slot = lax.broadcasted_iota(jnp.int32, (ROWS, TOKENS), 0).astype(F32)
    taken = [
        (slot == ids[pl.ds(p, 1), :].astype(F32) * CAP + jnp.sum(hot[p] * counts, axis=0, keepdims=True)).astype(F32)
        for p in range(2)
    ]
    chooser = (taken[0] + taken[1]).astype(BF16)
    blend = taken[0] * gates[pl.ds(0, 1), :] + taken[1] * gates[pl.ds(1, 1), :]
    blend_hi = blend.astype(BF16)
    blend_lo = (blend - blend_hi.astype(F32)).astype(BF16)
    xfloat = xc[...].astype(F32)
    gate = silu(gate_in[...].astype(F32))

    total = psend[tp].astype(F32)
    for i, c in enumerate(copies):
        c.wait_recv()
        total = total + precv[i].astype(F32)
    for c in copies:
        c.wait_send()
    pall[tp] = total.astype(BF16)
    copies = []
    for i, (dy, dx) in enumerate(PEERS):
        c = remote(pall.at[tp], pall.at[tp], a_send.at[i], a_recv.at[i], {"tp": peer_of(dy, dx)})
        c.start()
        copies.append(c)
    for c in copies:
        c.wait_send()
    for c in copies:
        c.wait_recv()
    projected = pall[...].astype(F32).reshape(TOKENS, RANK + 2 * STATE)
    rank_part = projected[:, :RANK].astype(BF16)
    maps = projected[:, RANK:]

    eye = (
        lax.broadcasted_iota(jnp.int32, (2 * STATE, 2 * STATE), 0) == lax.broadcasted_iota(jnp.int32, (2 * STATE, 2 * STATE), 1)
    ).astype(F32)
    spread = (maps[:, None, :] * eye[None]).reshape(TOKENS * 2 * STATE, 2 * STATE).astype(BF16)
    mb[...] = dot(spread, jnp.ones((2 * STATE, 128), BF16)).reshape(TOKENS, 2 * STATE, 128)

    raw = dot(rank_part, step_w[...]) + step_b[...]
    step_sizes = jnp.maximum(raw, 0.0) + jnp.log1p(jnp.exp(-jnp.abs(raw)))
    steps[...] = step_sizes
    driven[...] = step_sizes * xfloat
    decay = -jnp.exp(decay_log[...])
    send_state = remote(hend, hstart, ctx_send.at[1], ctx_recv.at[1], partner)

    @pl.when(core == 0)
    def _():
        hstart[...] = jnp.zeros_like(hstart)

    @pl.when(core == 1)
    def _():
        send_state.wait_recv()

    def scan_block(block, h):
        for i in range(8):
            t = block * 8 + i
            m = mb[t]
            in_map = jnp.concatenate([m[:STATE], m[:STATE]], axis=1)
            out_map = jnp.concatenate([m[STATE:], m[STATE:]], axis=1)
            h = jnp.exp(steps[pl.ds(t, 1), :] * decay) * h + driven[pl.ds(t, 1), :] * in_map
            ys[pl.ds(t, 1), :] = jnp.sum(out_map * h, axis=0, keepdims=True)
        return h

    hend[...] = lax.fori_loop(0, TOKENS // 8, scan_block, hstart[...])

    @pl.when(core == 0)
    def _():
        send_state.start()

    send_w = remote(experts, wv.at[1], ctx_send.at[2], ctx_recv.at[2], partner)
    send_w.start()
    gated = ((ys[...] + skip[...] * xfloat) * gate).astype(BF16)

    load_ow.wait()
    load_res.wait()
    copies = []

    def out_tiles(h, d):
        at, rows = lax.rem((my_y if h == 0 else my_x) + d, SIDE), pl.ds(h * 64, 64)
        return osend.at[at, :, rows, :] if h == 0 else osend.at[:, at, rows, :]

    def out_send(src, dst, phase, h, d):
        to = chip(h, 0, d) if phase == 0 else chip(h, d, 0)
        c = remote(src, dst.at[h, d - 1], o_send.at[phase, h, d - 1], o_recv.at[phase, h, d - 1], {"tp": to})
        c.start()
        copies.append(c)

    def out_arrived(buf, phase, h, d):
        ref = buf.at[h, d - 1]
        remote(ref, ref, o_send.at[phase, h, d - 1], o_recv.at[phase, h, d - 1], {"tp": tp}).wait_recv()
        return ref[...].astype(F32)

    for dy in (1, 3, 2, 0):
        yy = lax.rem(my_y + dy, SIDE)
        piece = dot(gated, ow[:, pl.ds(pl.multiple_of(yy * 512, 512), 512)])
        for j in range(SIDE):
            osend[yy, j] = piece[:, j * 128 : (j + 1) * 128].astype(BF16)
        if dy:
            out_send(out_tiles(0, dy), orecv, 0, 0, dy)
    for d in (1, 3, 2):
        out_send(out_tiles(1, d), orecv, 0, 1, d)
    for h in range(2):
        total = out_tiles(h, 0)[...].astype(F32)
        for d in range(1, SIDE):
            total = total + out_arrived(orecv, 0, h, d)
        ohalf[h] = total.astype(BF16)
        for d in (1, 3, 2):
            out_send(ohalf.at[h, lax.rem((my_x if h == 0 else my_y) + d, SIDE)], orecv2, 1, h, d)
    mixed = []
    for h in range(2):
        total = ohalf[h, my_x if h == 0 else my_y].astype(F32)
        for d in range(1, SIDE):
            total = total + out_arrived(orecv2, 1, h, d)
        mixed.append(total)
    mixed = jnp.concatenate(mixed, axis=0)
    stream = (res[...].astype(F32) + mixed).astype(BF16)

    chosen = dot(chooser, stream).astype(BF16).reshape(EXP, CAP, 128)
    picked[...] = chosen
    zcopies = [None] * EXP
    spread = []
    for unit in SPREAD:
        start, count, h = UNITS[unit]
        pos = start // CAP
        dest = lax.rem(z + EXP - NEAR[pos], EXP)
        for d in (1, 3, 2, 0):
            m = (d + 15) % 16 if d == 0 else d - 1
            c = remote(
                picked.at[dest, pl.ds(start - pos * CAP, count)],
                xs.at[pl.ds(start, count), my_lanes],
                g_send.at[unit, m],
                g_recv.at[unit, m],
                {"exp": dest, "tp": chip(h, d, 0)},
            )
            c.start()
            spread.append(c)
    for pos in range(4, EXP):
        dest = lax.rem(z + EXP - NEAR[pos], EXP)
        c = remote(picked.at[dest], xs.at[pl.ds(pos * CAP, CAP), my_lanes], z_send.at[pos], z_recv.at[pos], {"exp": dest})
        c.start()
        zcopies[pos] = c
    keep = pltpu.make_async_copy(picked.at[z], xs.at[pl.ds(0, CAP), my_lanes], local_sem.at[3])
    keep.start()
    keep.wait()
    sent = []
    FAR = (1, 3, 2)

    def gather(unit):
        start, count, h = UNITS[unit]
        rows = pl.ds(start, count)

        def part_of(du, dv):
            return xs.at[rows, pl.ds(pl.multiple_of(chip(h, du, dv) * 128, 128), 128)]

        def put(m, to, origin):
            ref = part_of(*origin)
            c = remote(ref, ref, g_send.at[unit, m], g_recv.at[unit, m], {"tp": chip(h, *to)})
            c.start()
            sent.append(c)

        def got(m, origin):
            ref = part_of(*origin)
            remote(ref, ref, g_send.at[unit, m], g_recv.at[unit, m], {"tp": tp}).wait_recv()

        if unit in SPREAD:
            got(15, (0, 0))
        else:
            for d in (1, 3, 2):
                put(d - 1, (d, 0), (0, 0))
        for d in FAR:
            put(3 + d - 1, (0, d), (0, 0))
        yield
        for u in (1, 3, 2):
            got(SIDE - u - 1, (u, 0))
            for d in FAR:
                put(3 + 3 * u + d - 1, (0, d), (u, 0))
            if u != 1:
                yield
        for u in range(SIDE):
            for d in FAR:
                got(3 + 3 * u + d - 1, (u, SIDE - d))
        yield

    def scatter(g, h):
        my_a, my_b = (my_y, my_x) if h == 0 else (my_x, my_y)

        def near(at, d):
            return lax.rem(at + d, SIDE)

        def tiles(d, q):
            rows = pl.ds(h * 128 + q * 64, 64)
            return rsend.at[g, near(my_a, d), :, rows, :] if h == 0 else rsend.at[g, :, near(my_a, d), rows, :]

        def lane(d, q):
            return half_sum.at[g, h, near(my_b, d), pl.ds(q * 64, 64), :]

        def arrived(buf, ss, rs, q, d):
            ref = buf.at[g, h, q, d - 1]
            remote(ref, ref, ss.at[g, h, q, d - 1], rs.at[g, h, q, d - 1], {"tp": tp}).wait_recv()
            return ref[...].astype(F32)

        for q, d in [(q, d) for q in range(2) for d in FAR]:
            c = remote(tiles(d, q), one.at[g, h, q, d - 1], r_send.at[g, h, q, d - 1], r_recv.at[g, h, q, d - 1], {"tp": chip(h, 0, d)})
            c.start()
            sent.append(c)
            yield
        for q in range(2):
            total = tiles(0, q)[...].astype(F32)
            for d in range(1, SIDE):
                total = total + arrived(one, r_send, r_recv, q, d)
            half_sum[g, h, :, pl.ds(q * 64, 64), :] = total.astype(BF16)
            for d in FAR:
                c = remote(lane(d, q), two.at[g, h, q, d - 1], q_send.at[g, h, q, d - 1], q_recv.at[g, h, q, d - 1], {"tp": chip(h, d, 0)})
                c.start()
                sent.append(c)
            yield
        for q in range(2):
            pos = g * 4 + h * 2 + q
            total = lane(0, q)[...].astype(F32)
            for d in range(1, SIDE):
                total = total + arrived(two, q_send, q_recv, q, d)
            rows = pl.ds(pos * CAP, CAP)
            ret_send[rows, :] = total.astype(BF16)
            dst = ret.at[pl.ds(pl.multiple_of(z * CAP, CAP), CAP)]
            k = NEAR[pos]
            if k:
                c = remote(ret_send.at[rows], dst, b_send.at[pos], b_recv.at[pos], {"exp": lax.rem(z + k, EXP)})
            else:
                c = pltpu.make_async_copy(ret_send.at[rows], dst, local_sem.at[4])
            c.start()
            bcopies[pos] = c
            yield

    bcopies = [None] * EXP
    gathers = [[gather(2 * i), gather(2 * i + 1)] for i in range(4)]
    scatters = [[scatter(g, h) for h in range(2)] for g in range(2)]

    def step(pair):
        for one_of in pair:
            next(one_of)

    def landed(*positions):
        for pos in positions:
            zcopies[pos].wait_recv()

    step(gathers[0])
    step(gathers[0])
    step(gathers[0])
    step(gathers[1])
    step(gathers[1])
    step(gathers[1])
    step(gathers[2])
    step(gathers[2])
    step(gathers[2])
    landed(4, 5, 6, 7)
    step(gathers[3])
    step(gathers[0])
    step(gathers[1])
    step(gathers[2])
    for c in copies:
        c.wait_send()
    load_wv.wait()

    def normalize(g):
        def norm_rows(r, _):
            rows = xs[pl.ds(pl.multiple_of(g * GROUP + r * 64, 64), 64), :].astype(F32)
            scale = lax.rsqrt(jnp.mean(rows * rows, axis=1, keepdims=True) + 1e-06)
            xn[pl.ds(pl.multiple_of(r * 64, 64), 64), :] = (rows * scale * gain[...]).astype(BF16)
            return 0

        lax.fori_loop(0, GROUP // 64, norm_rows, 0)

    def up(w):
        gate_part = dot(xn[...], wv[w, 0], ((1,), (1,)))
        up_part = dot(xn[...], wv[w, 1], ((1,), (1,)))
        hid[w] = (silu(gate_part) * up_part).astype(BF16)

    def down(g, dy):
        yy = lax.rem(my_y + dy, SIDE)
        cols = pl.ds(pl.multiple_of(yy * 512, 512), 512)
        piece = dot(hid[0], wv[0, 2, :, cols]) + dot(hid[1], wv[1, 2, :, cols])
        for j in range(SIDE):
            rsend[g, yy, j] = piece[:, j * 128 : (j + 1) * 128].astype(BF16)

    def all_down(g):
        for dy in (1, 3, 2, 0):
            down(g, dy)
            if dy:
                next(scatters[g][0])
        for h in (1, 0, 1):
            for _ in range(3):
                next(scatters[g][h])

    normalize(0)
    step(gathers[3])
    send_w.wait_recv()
    up(0)
    step(gathers[3])
    up(1)
    all_down(0)
    step(gathers[3])
    normalize(1)
    up(0)
    up(1)
    step(scatters[0])
    all_down(1)
    step(scatters[0])
    step(scatters[1])
    step(scatters[1])
    step(scatters[0])
    step(scatters[0])
    step(scatters[1])
    step(scatters[1])
    for pos, c in enumerate(bcopies):
        if NEAR[pos]:
            c.wait_recv()
        else:
            c.wait()
    back = ret[...]
    moe = dot(blend_hi, back, ((0,), (0,))) + dot(blend_lo, back, ((0,), (0,)))
    out[...] = (stream.astype(F32) + moe).astype(BF16)

    @pl.when(core == 0)
    def _():
        send_halo.wait_send()
        send_state.wait_send()

    send_w.wait_send()
    for c in zcopies[4:] + spread + sent:
        c.wait_send()
    for pos, c in enumerate(bcopies):
        if NEAR[pos]:
            c.wait_send()


def body(
    conv_in, gate_in, residual, conv_weight, conv_bias, proj_weight, step_weight, step_bias, decay_log, skip_gain, out_weight, norm_gain,
    expert_ids, route_gates, expert_weight,
):
    vmem, hbm = pl.BlockSpec(memory_space=pltpu.VMEM), pl.BlockSpec(memory_space=pl.ANY)
    dma, n = pltpu.SemaphoreType.DMA, len(PEERS)
    wide = RANK + 2 * STATE
    result = pl.pallas_call(
        kernel,
        out_shape=jax.ShapeDtypeStruct((TOKENS, 128), BF16),
        in_specs=[hbm] * 15,
        out_specs=vmem,
        scratch_shapes=[
            pltpu.VMEM((TOKENS, CHANNELS), BF16),
            pltpu.VMEM((TOKENS, CHANNELS), BF16),
            pltpu.VMEM((4, CHANNELS), F32),
            pltpu.VMEM((1, CHANNELS), F32),
            pltpu.VMEM((wide, CHANNELS), BF16),
            pltpu.VMEM((RANK, CHANNELS), BF16),
            pltpu.VMEM((1, CHANNELS), F32),
            pltpu.VMEM((STATE, CHANNELS), F32),
            pltpu.VMEM((1, CHANNELS), F32),
            pltpu.VMEM((1, D), F32),
            pltpu.VMEM((2, TOKENS), jnp.int32),
            pltpu.VMEM((2, TOKENS), F32),
            pltpu.VMEM((TOKENS, CHANNELS), BF16),
            pltpu.VMEM((16, CHANNELS), BF16),
            pltpu.VMEM((TOKENS + 8, CHANNELS), F32),
            pltpu.VMEM((TP, 8, wide), BF16),
            pltpu.VMEM((n, 8, wide), BF16),
            pltpu.VMEM((TP, 8, wide), BF16),
            pltpu.VMEM((TOKENS, 2 * STATE, 128), F32),
            pltpu.VMEM((TOKENS, CHANNELS), F32),
            pltpu.VMEM((TOKENS, CHANNELS), F32),
            pltpu.VMEM((TOKENS, CHANNELS), F32),
            pltpu.VMEM((STATE, CHANNELS), F32),
            pltpu.VMEM((STATE, CHANNELS), F32),
            pltpu.VMEM((CHANNELS, D), BF16),
            pltpu.VMEM((TOKENS, 128), BF16),
            pltpu.VMEM((SIDE, SIDE, TOKENS, 128), BF16),
            pltpu.VMEM((2, 3, SIDE, 64, 128), BF16),
            pltpu.VMEM((2, SIDE, 64, 128), BF16),
            pltpu.VMEM((2, 3, 64, 128), BF16),
            pltpu.VMEM((EXP, CAP, 128), BF16),
            pltpu.VMEM((ROWS, D), BF16),
            pltpu.VMEM((GROUP, D), BF16),
            pltpu.VMEM((2, 3, HIDDEN, D), BF16),
            pltpu.VMEM((2, GROUP, HIDDEN), BF16),
            pltpu.VMEM((2, SIDE, SIDE, GROUP, 128), BF16),
            pltpu.VMEM((2, 2, 2, 3, SIDE, 64, 128), BF16),
            pltpu.VMEM((2, 2, SIDE, 128, 128), BF16),
            pltpu.VMEM((2, 2, 2, 3, 64, 128), BF16),
            pltpu.VMEM((ROWS, 128), BF16),
            pltpu.VMEM((ROWS, 128), BF16),
            dma((12,)), dma((5,)), dma((3,)), dma((3,)),
            dma((n,)), dma((n,)), dma((n,)), dma((n,)), dma((2, 2, 3)), dma((2, 2, 3)),
            dma((EXP,)), dma((EXP,)),
            dma((len(UNITS), 16)), dma((len(UNITS), 16)),
            dma((2, 2, 2, 3)), dma((2, 2, 2, 3)), dma((2, 2, 2, 3)), dma((2, 2, 2, 3)),
            dma((EXP,)), dma((EXP,)),
        ],
        compiler_params=pltpu.CompilerParams(collective_id=0, has_side_effects=True, vmem_limit_bytes=60 << 20),
        name="mixer_experts",
    )(
        conv_in[0], gate_in[0], residual[0], conv_weight, conv_bias[None], proj_weight.T, step_weight, step_bias[None], decay_log,
        skip_gain[None], out_weight, norm_gain[None], expert_ids[0].T, route_gates[0].T,
        jnp.swapaxes(expert_weight[0], 1, 2),
    )
    return result[None]


def solution(mesh):
    placed = (
        P("exp", "ctx", "tp"),
        P("exp", "ctx", "tp"),
        P("exp", "ctx", None),
        P(None, "tp"),
        P("tp"),
        P("tp", None),
        P(None, "tp"),
        P("tp"),
        P(None, "tp"),
        P("tp"),
        P("tp", None),
        P(),
        P("exp", "ctx", None),
        P("exp", "ctx", None),
        P("exp", None, None, ("ctx", "tp")),
    )
    return jax.shard_map(body, mesh=mesh, in_specs=placed, out_specs=P("exp", "ctx", "tp"), check_vma=False)
```
